32 devices in a mesh: groups: 2 (over y), sub: 4 (over z), rhs: 2 (over x), face: 2 (over core).
Axes of the slice: x: 2, y: 2, z: 4, core: 2. Of those that a mesh axis runs over, the one named last changes fastest.
Arguments:
- mortar_in: bfloat16 [1024, 64, 256], P(('groups', 'sub'), 'rhs'), parts along dimension 0, may hold values from -6 to 6
- pump_rate: float32 [128], P(('groups', 'rhs')), parts along dimension 0, may hold values from 4 to 16
- well_cell: int32 [128], P(('groups', 'rhs')), parts along dimension 0, may hold values from 0 to 131071
- face_owner: int32 [2048, 1], P(('groups', 'sub', 'face')), parts along dimension 0, may hold values from 0 to 3; in each aligned block of 128 rows (0 to 127, 128 to 255, ...) at most 64 rows name the same one
- face_slot: int32 [2048], P(('groups', 'sub', 'face')), parts along dimension 0, may hold values from 0 to 127
- face_scale: bfloat16 [2048, 256], P(('groups', 'sub', 'face')), parts along dimension 0, may hold values from 0.5 to 2
- section: int32 [8], P(('groups', 'sub')), parts along dimension 0, may hold values 0 or 1
- basis: bfloat16 [8, 256, 256], P(('groups', 'sub')), parts along dimension 0, may hold values from -0.375 to 0.375
- projection: bfloat16 [256, 256], replicated, may hold values from -0.375 to 0.375
Outputs:
- result: float32 [1024, 64, 256], P(('groups', 'sub', 'face'), 'rhs'), parts along dimension 0
The draws below stay inside these ranges and needn't reach their ends.
There are 2 independent parts, one for each index of `groups`. The reference program is written for one: setup_inputs(seed, part) draws one part's arguments, and reference() takes and returns one part's arrays. A program takes and returns all parts, laid end to end along the dimension named above; an argument that names none is the same for every part. Nothing has to cross between parts.
Inputs may be any that keep to these rules, and one draw needn't show every extreme that they name: `face_owner`: among the 128 faces of one device no subdomain is named by more than 64 faces, a bound that some block reaches.
All inputs are finite; a program needn't handle non-finite values. No bound on the sum of `section` on one device may be relied on, other than what follows from the above.
Results may differ from the reference program's by a relative error of at most 0.004.
Values may be sent and summed in bfloat16 or wider, within the bound.
A program may use at most 64 MiB of HBM per device.

```python
import math
import jax
import jax.numpy as jnp
import numpy as np
from jax import lax

K = 256
COLS = 64
F_DEV = 128
SUBS = 4
MB_DEV = 128
MBLK = 512
FACES = 1024
CAP = 64
N_FACE = 2


def with_ends(entries, rng, smallest, high):
    longest = entries.shape.index(max(entries.shape))
    spots = []
    for shift in (0, 1):
        where = [jax.random.randint(jax.random.fold_in(rng, axis), (), 0, length) for axis, length in enumerate(entries.shape)]
        where[longest] = (where[longest] + shift) % entries.shape[longest]
        spots.append(tuple(where))
    return entries.at[spots[0]].set(smallest).at[spots[1]].set(high)


def block_scale(rng, extent, cuts, smallest, high):
    level, own = 1.0, jax.random.fold_in(rng, 6)
    for axis_at, shards_of in cuts:
        steps = jnp.exp(jax.random.uniform(jax.random.fold_in(own, axis_at), (shards_of,), jnp.float32, smallest / len(cuts), high / len(cuts)))
        level = level * jnp.repeat(steps, extent[axis_at] // shards_of).reshape([-1 if axis == axis_at else 1 for axis in range(len(extent))])
    return level


def assign_block(key, own, number, rows, number_of, top, limit, slope):
    order = jax.random.permutation(key, number_of)
    crowded, ordinary = shares(number_of, rows * top, limit, slope, True), shares(number_of, rows * top, limit, slope, False)
    places = jnp.arange(number_of)

    def named(tallies, rotation):
        used = int((tallies > 0).sum())
        fixed = max(1, used // 4)
        shifted = fixed + (places - fixed + rotation * (used - fixed)) % max(1, number_of - fixed)
        return jnp.zeros((number_of,), jnp.int32).at[order[jnp.where(places < fixed, places, shifted)]].set(jnp.asarray(tallies, jnp.int32))

    tallies = jnp.where(number % 4 == 0, named(crowded, number // 4), named(ordinary, number - number // 4 - 1))
    mixed = jax.random.permutation(jax.random.fold_in(own, 3), number_of)
    source_of, receiver = mixed[0:number_of // 2 * 2:2], mixed[1:number_of // 2 * 2:2]
    room = jnp.minimum(tallies[source_of] - 1, limit - tallies[receiver]) // 2
    room = jnp.where((source_of == order[0]) | (receiver == order[0]) | (tallies[receiver] == 0), 0, jnp.maximum(room, 0))
    shifted = jax.random.randint(jax.random.fold_in(own, 4), (number_of // 2,), 0, 1 << 20) % (room + 1)
    tallies = tallies.at[source_of].add(-shifted).at[receiver].add(shifted)
    members = jnp.searchsorted(jnp.cumsum(tallies), jnp.arange(rows * top), side="right").astype(jnp.int32)
    table = members.reshape(top, rows).T
    table = table[jax.random.permutation(jax.random.fold_in(own, 1), rows)]
    rotation = jax.random.randint(jax.random.fold_in(own, 2), (rows, 1), 0, top)
    return jnp.take_along_axis(table, (jnp.arange(top)[None, :] + rotation) % top, axis=1)


def shares(amount, total, bound, skew, full):
    loads = [(1 << 20) // math.isqrt(rank ** skew) + 1 for rank in range(1, amount + 1)]
    largest = bound if full else min(bound, max(-(-total // amount), total * loads[0] // sum(loads)))
    least = 1 if total - largest >= amount - 1 else 0
    given, surplus = [largest] + [least] * (amount - 1), total - largest - least * (amount - 1)
    while surplus > 0:
        movable = [i for i in range(1, amount) if given[i] < largest] or [i for i in range(1, amount) if given[i] < bound]
        whole, remaining = sum([loads[i] for i in movable]), surplus
        for i in movable:
            addition = min(bound - given[i], max(1, remaining * loads[i] // whole), surplus)
            given[i] = given[i] + addition
            surplus = surplus - addition
    return np.array(given)


def gaussian(key, shape, spread, most, pieces=(), kind=jnp.bfloat16):
    array = jax.random.normal(key, shape, jnp.float32) * spread
    if len(pieces) > 0:
        array = block_scale(key, shape, pieces, -0.22, 0.18) * array
    return jnp.clip(array, min=-most, max=most).astype(kind)


def setup_inputs(seed: int = 0, part: int = 0) -> dict:
    key_list = jax.random.split(jax.random.key(seed), 10)
    own_keys = jax.random.split(jax.random.fold_in(key_list[9], part), 10)
    mortar_in = gaussian(own_keys[0], (MBLK, COLS, K), 1.0, 6.0, ((0, 4), (1, 2)))
    pump_rate = jnp.clip(jnp.exp(math.log(16.0) - 1.3862944 * jax.random.uniform(own_keys[1], (COLS,), jnp.float32) ** block_scale(own_keys[1], (COLS,), ((0, 2),), -0.2, 0.2)), 4.0, 16.0)
    well_cell = with_ends(jax.random.randint(own_keys[2], (COLS,), 0, MBLK * K), jax.random.fold_in(own_keys[2], 1), 0, (MBLK * K) - 1).astype(jnp.int32)
    face_owner_keys = jax.random.split(jax.random.fold_in(own_keys[3], 1), FACES // F_DEV)
    face_owner_turns = jax.random.permutation(jax.random.fold_in(own_keys[3], 3), FACES // F_DEV)
    face_owner = jax.vmap(lambda own, number: assign_block(jax.random.fold_in(own_keys[3], 2), own, number, F_DEV, SUBS, 1, CAP, 2))(face_owner_keys, face_owner_turns).reshape((FACES, 1))
    face_slot = with_ends(jax.random.randint(own_keys[4], (FACES,), 0, MB_DEV), jax.random.fold_in(own_keys[4], 1), 0, MB_DEV - 1).astype(jnp.int32)
    face_scale = jnp.clip(jnp.exp(math.log(2.0) - 1.3862944 * jax.random.uniform(own_keys[5], (FACES, K), jnp.float32) ** block_scale(own_keys[5], (FACES, K), ((0, 8),), -0.2, 0.2)), 0.5, 2.0).astype(jnp.bfloat16)
    section = with_ends((jax.random.randint(own_keys[6], (SUBS,), 0, 4) < 1).astype(jnp.int32), jax.random.fold_in(own_keys[6], 1), 0, 1)
    basis = gaussian(own_keys[7], (SUBS, K, K), K ** -0.5, 0.375, ((0, 4),))
    projection = gaussian(key_list[8], (K, K), K ** -0.5, 0.375)
    return {"mortar_in": mortar_in, "pump_rate": pump_rate, "well_cell": well_cell, "face_owner": face_owner, "face_slot": face_slot, "face_scale": face_scale, "section": section, "basis": basis, "projection": projection}


def reference(mortar_in, pump_rate, well_cell, face_owner, face_slot, face_scale, section, basis, projection):
    columns = jnp.arange(COLS, dtype=jnp.int32)
    well_terms = jnp.zeros((MBLK, COLS, K), jnp.float32).at[well_cell // K, columns, well_cell % K].add(pump_rate)
    pumped = (mortar_in.astype(jnp.float32) + well_terms).astype(jnp.bfloat16)
    wanted = (face_owner[:, 0] * MB_DEV + face_slot).astype(jnp.int32)
    face_values = pumped[wanted]
    scaled = (face_values.astype(jnp.float32) * face_scale.astype(jnp.float32)[:, None, :]).astype(jnp.bfloat16)
    grouped = scaled.reshape(SUBS, F_DEV * N_FACE * COLS, K)
    signs = (1 - 2 * section).astype(jnp.float32)

    def one_subdomain(items):
        rows, local_basis, orient = items
        return jnp.dot(rows, local_basis, preferred_element_type=jnp.float32) * orient

    flux_rows = lax.map(one_subdomain, (grouped, basis, signs)).reshape(FACES, COLS, K)
    summed = jax.ops.segment_sum(flux_rows, wanted, num_segments=MBLK)
    summed_low = summed.astype(jnp.bfloat16).reshape(MBLK * COLS, K)
    result = jnp.dot(summed_low, projection, preferred_element_type=jnp.float32)
    return result.reshape(MBLK, COLS, K)
```

```python
import functools

import jax
import jax.numpy as jnp
from jax import lax
from jax.experimental import pallas as pl
from jax.experimental.pallas import tpu as pltpu
from jax.sharding import PartitionSpec as P

MESH = pl.DeviceIdType.MESH
F32, BF16 = jnp.float32, jnp.bfloat16
BASIS, SCALE, CODE = 0, 1, 2


def row_to_column(row, length):
    rows = lax.broadcasted_iota(jnp.int32, (length, length), 0)
    lanes = lax.broadcasted_iota(jnp.int32, (length, length), 1)
    spread = jnp.broadcast_to(row, (length, length))
    return jnp.sum(jnp.where(rows == lanes, spread, 0.0), axis=1, keepdims=True)


def kernel(
    sizes,
    owner_hbm, slot_hbm, section_hbm, cell_hbm, rate_hbm, mortar_ref, scale_ref, basis_ref,
    projection_ref,
    total, weights, pumped, basis_last, projection_out,
    owner_ref, slot_ref, section_ref, cell_ref, rate_ref,
    scale_in, packed, codes_out, bases, scales, codes,
    local_sems, swap_send, swap_recv,
    z_send, z_recv, x_send, x_recv, core_send, core_recv,
):
    subs, width, faces, blocks, cols, dofs, room = sizes
    me_z, me_x, me_f = lax.axis_index("sub"), lax.axis_index("rhs"), lax.axis_index("face")
    half = blocks // 2
    other_f = 1 - me_f
    shares = (dofs // (2 * width), room // width)

    low = 1 - (2 * me_z) // subs
    margin = low * me_z + (1 - low) * (subs - 1 - me_z)

    def by_distance(k):
        beyond = (k - 2 * margin - 1 + 4 * subs) // (4 * subs)
        side = (1 - beyond) * (2 * (k % 2) - 1) + beyond * (2 * low - 1)
        reach = (1 - beyond) * ((k + 1) // 2) + beyond * (k - margin)
        return me_z + side * reach

    def in_turn(k):
        return (k - 1) + (k - 1 + subs - me_z) // subs

    def part(z, x, f, kind):
        if kind == CODE:
            return codes.at[z, f]
        share = shares[kind]
        at = pl.ds(pl.multiple_of((f * width + x) * share, share), share)
        return (bases if kind == BASIS else scales).at[z, at, :]

    def remote(src, dst, send, recv, device):
        return pltpu.make_async_remote_copy(
            src_ref=src, dst_ref=dst, send_sem=send, recv_sem=recv,
            device_id=device, device_id_type=MESH,
        )

    load_basis = pltpu.make_async_copy(basis_ref.at[0], bases.at[me_z], local_sems.at[0])
    load_scale = pltpu.make_async_copy(scale_ref, scale_in, local_sems.at[1])
    load_mortar = pltpu.make_async_copy(
        mortar_ref.at[pl.ds(me_f * half, half)], pumped, local_sems.at[2]
    )
    load_projection = pltpu.make_async_copy(projection_ref, projection_out, local_sems.at[3])
    small = [
        pltpu.make_async_copy(src, dst, local_sems.at[4 + i])
        for i, (src, dst) in enumerate((
            (owner_hbm, owner_ref), (slot_hbm, slot_ref), (section_hbm, section_ref),
            (cell_hbm, cell_ref), (rate_hbm, rate_ref),
        ))
    ]
    for copy in small[:3]:
        copy.start()
    load_basis.start()
    load_scale.start()
    barrier = pltpu.get_barrier_semaphore()
    pl.semaphore_signal(barrier, inc=1, device_id={"face": other_f}, device_id_type=MESH)
    for dx in range(1, width):
        pl.semaphore_signal(
            barrier, inc=1, device_id={"rhs": lax.rem(me_x + dx, width)}, device_id_type=MESH
        )
    for dz in range(1, subs):
        pl.semaphore_signal(
            barrier, inc=1, device_id={"sub": lax.rem(me_z + dz, subs)}, device_id_type=MESH
        )
    for copy in small[3:]:
        copy.start()
    load_mortar.start()
    load_projection.start()

    for copy in small[:3]:
        copy.wait()
    load_scale.wait()

    owner = owner_ref[...]
    lanes = lax.broadcasted_iota(jnp.int32, (faces, faces), 1)
    rows = lax.broadcasted_iota(jnp.int32, (faces, faces), 0)
    earlier = jnp.where(rows < lanes, 1.0, 0.0).astype(BF16)
    padded = -(-subs // 16) * 16
    named = lax.broadcasted_iota(jnp.int32, (padded, faces), 0) == jnp.broadcast_to(
        owner, (padded, faces)
    )
    named = jnp.where(named, 1.0, 0.0)
    ranks = jnp.dot(named.astype(BF16), earlier, preferred_element_type=F32)
    rank = jnp.sum(named * ranks, axis=0, keepdims=True).astype(jnp.int32)
    sign = (1 - 2 * section_ref[0]).astype(F32)
    place = lax.broadcasted_iota(jnp.int32, (subs * room, faces), 0) == jnp.broadcast_to(
        owner * room + rank, (subs * room, faces)
    )
    packed[...] = jnp.dot(
        jnp.where(place, sign, 0.0).astype(BF16), scale_in[...], preferred_element_type=F32
    ).astype(BF16)
    spot = lax.broadcasted_iota(jnp.int32, (subs * 2 * room, faces), 0) == jnp.broadcast_to(
        (owner * 2 + me_f) * room + rank, (subs * 2 * room, faces)
    )
    slots = jnp.broadcast_to((slot_ref[...] + 1).astype(F32), (16, faces)).astype(BF16)
    coded = lax.dot_general(
        slots, jnp.where(spot, 1.0, 0.0).astype(BF16), (((1,), (1,)), ((), ())),
        preferred_element_type=F32,
    )
    for d in range(subs):
        codes_out[d] = coded[:1, d * 2 * room:(d + 1) * 2 * room]
    load_basis.wait()
    pl.semaphore_wait(barrier, subs + width - 1)

    sends = []

    def start(copy):
        sends.append(copy)
        copy.start()

    for k in reversed(range(1, subs)):
        d = by_distance(k)
        start(remote(
            part(me_z, me_x, me_f, BASIS), part(me_z, me_x, me_f, BASIS),
            z_send.at[k, BASIS], z_recv.at[me_z, BASIS], {"sub": d},
        ))
        share = shares[SCALE]
        mine = packed.at[pl.ds(pl.multiple_of(d * room + me_x * share, share), share), :]
        start(remote(
            mine, part(me_z, me_x, me_f, SCALE),
            z_send.at[k, SCALE], z_recv.at[me_z, SCALE], {"sub": d},
        ))
        start(remote(
            codes_out.at[d], codes.at[me_z, me_f],
            z_send.at[k, CODE], z_recv.at[me_z, CODE], {"sub": d},
        ))
    own_rows = pl.ds(pl.multiple_of(me_z * room, room), room)

    def own_part(f):
        return scales.at[me_z, pl.ds(pl.multiple_of(f * room, room), room), :]

    start(remote(
        packed.at[own_rows, :], own_part(me_f), swap_send.at[0], swap_recv.at[0],
        {"face": other_f},
    ))
    start(remote(
        codes_out.at[me_z], codes.at[me_z, me_f], swap_send.at[1], swap_recv.at[1],
        {"face": other_f},
    ))
    scales[me_z, pl.ds(pl.multiple_of(me_f * room, room), room), :] = packed[own_rows, :]
    codes[me_z, me_f] = codes_out[me_z]

    first = me_z * blocks + me_f * half
    for copy in small[3:]:
        copy.wait()
    load_mortar.wait()
    cell = row_to_column(cell_ref[...].astype(F32), cols).astype(jnp.int32)
    rate = row_to_column(rate_ref[...], cols)
    offset = (
        jnp.broadcast_to(cell, (cols, dofs))
        - lax.broadcasted_iota(jnp.int32, (cols, dofs), 1)
        - first * dofs
    )
    rates = jnp.broadcast_to(rate, (cols, dofs))

    @pl.loop(0, half)
    def _(b):
        term = jnp.where(offset == b * dofs, rates, 0.0)
        pumped[b] = (pumped[b].astype(F32) + term).astype(BF16)

    step = min(16, half)

    def weigh(z):
        code = jnp.broadcast_to(codes[z, 0] + codes[z, 1], (half, 2 * room)).astype(jnp.int32)
        targets = me_f * half + 1 + lax.broadcasted_iota(jnp.int32, (half, 2 * room), 0)
        picks = jnp.where(code == targets, 1.0, 0.0).astype(BF16)
        weights[...] = jnp.dot(picks, scales[z], preferred_element_type=F32)

    def compute(z, opening):
        weigh(z)

        @pl.loop(0, half // step)
        def _(i):
            rows = []
            for j in range(step):
                b = i * step + j
                rows.append((pumped[b].astype(F32) * weights[pl.ds(b, 1), :]).astype(BF16))
            flux = jnp.dot(
                jnp.concatenate(rows, axis=0), bases[z], preferred_element_type=F32
            )
            at = pl.ds(pl.multiple_of(i * (step * cols), step * cols), step * cols)
            if not opening:
                flux = flux + total[at, :]
            total[at, :] = flux

    remote(
        own_part(other_f), own_part(other_f), swap_send.at[0], swap_recv.at[0], {"face": other_f}
    ).wait_recv()
    theirs = codes.at[me_z, other_f]
    remote(theirs, theirs, swap_send.at[1], swap_recv.at[1], {"face": other_f}).wait_recv()
    compute(me_z, True)

    kinds = (BASIS, SCALE, CODE)

    def pass_on_z(k):
        z = in_turn(k)
        for kind in kinds:
            mine = part(z, me_x, me_f, kind)
            remote(
                mine, mine, core_send.at[z, me_x, kind], z_recv.at[z, kind], {"face": other_f}
            ).wait_recv()
            if kind != CODE:
                for dx in range(1, width):
                    x = lax.rem(me_x + dx, width)
                    start(remote(
                        mine, mine, x_send.at[z, x, kind], x_recv.at[z, me_x, kind], {"rhs": x}
                    ))
            start(remote(
                mine, mine, core_send.at[z, me_x, kind], core_recv.at[z, me_x, kind],
                {"face": other_f},
            ))

    def pass_on_x(k):
        z = in_turn(k)
        for kind in kinds[:2]:
            for dx in range(1, width):
                x = lax.rem(me_x + width - dx, width)
                came = part(z, x, me_f, kind)
                remote(
                    came, came, x_send.at[z, x, kind], x_recv.at[z, x, kind], {"face": other_f}
                ).wait_recv()
                start(remote(
                    came, came, core_send.at[z, x, kind], core_recv.at[z, x, kind],
                    {"face": other_f},
                ))

    def arrive(k):
        z = in_turn(k)
        for kind in kinds:
            for dx in range(width if kind != CODE else 1):
                x = lax.rem(me_x + dx, width)
                came = part(z, x, other_f, kind)
                remote(
                    came, came, core_send.at[z, x, kind], core_recv.at[z, x, kind],
                    {"face": other_f},
                ).wait_recv()
        return z

    for k in range(1, subs):
        pass_on_z(k)
    for k in range(1, subs):
        pass_on_x(k)
        if k > 1:
            compute(arrive(k - 1), False)
    last = arrive(subs - 1)
    weigh(last)
    basis_last[...] = bases[last]
    load_projection.wait()
    for copy in sends:
        copy.wait_send()


def project(total, weights, pumped, basis_ref, projection_ref, out_ref, staged, sems):
    parts, tile, _ = staged.shape
    cols = pumped.shape[1]
    step = tile // cols
    copies = []
    for i in range(parts):
        at = pl.ds(i * tile, tile)
        rows = []
        for j in range(step):
            b = i * step + j
            rows.append((pumped[b].astype(F32) * weights[pl.ds(b, 1), :]).astype(BF16))
        summed = total[at, :] + jnp.dot(
            jnp.concatenate(rows, axis=0), basis_ref[...], preferred_element_type=F32
        )
        staged[i] = jnp.dot(
            summed.astype(BF16), projection_ref[...], preferred_element_type=F32
        )
        copies.append(pltpu.make_async_copy(staged.at[i], out_ref.at[at], sems.at[i]))
        copies[-1].start()
    for copy in copies:
        copy.wait()


def on_device(
    mortar_in, pump_rate, well_cell, face_owner, face_slot, face_scale, section, basis, projection
):
    blocks, cols, dofs = mortar_in.shape
    faces = face_slot.shape[0]
    subs, width = lax.axis_size("sub"), lax.axis_size("rhs")
    half = blocks // 2
    cap = min(faces, -(-2 * faces // subs))
    share = -(-cap // (16 * width)) * 16
    room = share * width
    assert subs > 1 and blocks < 256
    sizes = (subs, width, faces, blocks, cols, dofs, room)
    vmem = pl.BlockSpec(memory_space=pltpu.VMEM)
    hbm = pl.BlockSpec(memory_space=pl.ANY)
    dma = pltpu.SemaphoreType.DMA
    kept = pl.pallas_call(
        functools.partial(kernel, sizes),
        out_shape=(
            pltpu.VMEM((half * cols, dofs), F32),
            pltpu.VMEM((half, dofs), F32),
            pltpu.VMEM((half, cols, dofs), BF16),
            pltpu.VMEM((dofs, dofs), BF16),
            pltpu.VMEM((dofs, dofs), BF16),
        ),
        in_specs=[hbm] * 9,
        out_specs=(vmem,) * 5,
        scratch_shapes=[
            pltpu.VMEM((1, faces), jnp.int32),
            pltpu.VMEM((1, faces), jnp.int32),
            pltpu.SMEM((1,), jnp.int32),
            pltpu.VMEM((1, cols), jnp.int32),
            pltpu.VMEM((1, cols), F32),
            pltpu.VMEM((faces, dofs), BF16),
            pltpu.VMEM((subs * room, dofs), BF16),
            pltpu.VMEM((subs, 1, 2 * room), F32),
            pltpu.VMEM((subs, dofs, dofs), BF16),
            pltpu.VMEM((subs, 2 * room, dofs), BF16),
            pltpu.VMEM((subs, 2, 1, 2 * room), F32),
            dma((9,)),
            dma((2,)), dma((2,)),
            dma((subs, 3)), dma((subs, 3)),
            dma((subs, width, 2)), dma((subs, width, 2)),
            dma((subs, width, 3)), dma((subs, width, 3)),
        ],
        compiler_params=pltpu.CompilerParams(collective_id=0, has_side_effects=True),
    )(
        face_owner.reshape(1, faces), face_slot.reshape(1, faces), section,
        well_cell.reshape(1, cols), pump_rate.reshape(1, cols), mortar_in, face_scale, basis,
        projection,
    )
    rows = half * cols
    parts = 8
    result = pl.pallas_call(
        project,
        out_shape=jax.ShapeDtypeStruct((rows, dofs), F32),
        in_specs=[vmem] * 5,
        out_specs=hbm,
        scratch_shapes=[pltpu.VMEM((parts, rows // parts, dofs), F32), dma((parts,))],
    )(*(pltpu.with_memory_space_constraint(a, pltpu.VMEM) for a in kept))
    return result.reshape(half, cols, dofs)


def solution(mesh):
    in_specs = (
        P(("groups", "sub"), "rhs", None),
        P(("groups", "rhs")),
        P(("groups", "rhs")),
        P(("groups", "sub", "face"), None),
        P(("groups", "sub", "face")),
        P(("groups", "sub", "face"), None),
        P(("groups", "sub")),
        P(("groups", "sub"), None, None),
        P(),
    )
    out_specs = P(("groups", "sub", "face"), "rhs", None)
    return jax.shard_map(
        on_device, mesh=mesh, in_specs=in_specs, out_specs=out_specs, check_vma=False
    )
```

```python
import functools

import jax
import jax.numpy as jnp
from jax import lax
from jax.experimental import pallas as pl
from jax.experimental.pallas import tpu as pltpu
from jax.sharding import PartitionSpec as P

MESH = pl.DeviceIdType.MESH
F32, BF16 = jnp.float32, jnp.bfloat16
BASIS, SCALE, CODE = 0, 1, 2


def row_to_column(row, length):
    rows = lax.broadcasted_iota(jnp.int32, (length, length), 0)
    lanes = lax.broadcasted_iota(jnp.int32, (length, length), 1)
    spread = jnp.broadcast_to(row, (length, length))
    return jnp.sum(jnp.where(rows == lanes, spread, 0.0), axis=1, keepdims=True)


def kernel(
    sizes,
    owner_hbm, slot_hbm, section_hbm, cell_hbm, rate_hbm, mortar_ref, scale_ref, basis_ref,
    projection_ref,
    total, weights, pumped, basis_last, projection_out,
    owner_ref, slot_ref, section_ref, cell_ref, rate_ref,
    scale_in, packed, codes_out, bases, scales, codes,
    local_sems, sent, swap_sent, swap_recv, z_recv, x_recv, core_recv, go_up, go_down,
):
    subs, width, faces, blocks, cols, dofs, room = sizes
    me_z, me_x, me_f = lax.axis_index("sub"), lax.axis_index("rhs"), lax.axis_index("face")
    half = blocks // 2
    other_f = 1 - me_f
    shares = (dofs // (2 * width), room // width)

    def inside(z):
        return jnp.logical_and(z >= 0, z < subs)

    def in_turn(k):
        return (k - 1) + (k - 1 + subs - me_z) // subs

    def turn(z, at):
        return z - (z + subs - 1 - at) // subs

    def part(z, x, f, kind):
        if kind == CODE:
            return codes.at[z, f]
        share = shares[kind]
        at = pl.ds(pl.multiple_of((f * width + x) * share, share), share)
        return (bases if kind == BASIS else scales).at[z, at, :]

    def remote(src, dst, send, recv, device):
        return pltpu.make_async_remote_copy(
            src_ref=src, dst_ref=dst, send_sem=send, recv_sem=recv,
            device_id=device, device_id_type=MESH,
        )

    load_basis = pltpu.make_async_copy(basis_ref.at[0], bases.at[me_z], local_sems.at[0])
    load_scale = pltpu.make_async_copy(scale_ref, scale_in, local_sems.at[1])
    load_mortar = pltpu.make_async_copy(
        mortar_ref.at[pl.ds(me_f * half, half)], pumped, local_sems.at[2]
    )
    load_projection = pltpu.make_async_copy(projection_ref, projection_out, local_sems.at[3])
    small = [
        pltpu.make_async_copy(src, dst, local_sems.at[4 + i])
        for i, (src, dst) in enumerate((
            (owner_hbm, owner_ref), (slot_hbm, slot_ref), (section_hbm, section_ref),
            (cell_hbm, cell_ref), (rate_hbm, rate_ref),
        ))
    ]
    for copy in small[:3]:
        copy.start()
    load_basis.start()
    load_scale.start()
    barrier = pltpu.get_barrier_semaphore()
    pl.semaphore_signal(barrier, inc=1, device_id={"face": other_f}, device_id_type=MESH)
    for dx in range(1, width):
        pl.semaphore_signal(
            barrier, inc=1, device_id={"rhs": lax.rem(me_x + dx, width)}, device_id_type=MESH
        )
    for z in (me_z - 1, me_z + 1):
        @pl.when(inside(z))
        def _():
            pl.semaphore_signal(barrier, inc=1, device_id={"sub": z}, device_id_type=MESH)
    for copy in small[3:]:
        copy.start()
    load_mortar.start()
    load_projection.start()

    neighbours = (me_z + subs - 1) // subs + (2 * subs - 2 - me_z) // subs
    pl.semaphore_wait(barrier, width + neighbours)
    if subs > 2:
        @pl.when(jnp.logical_and(me_z >= 1, me_z + 1 < subs))
        def _():
            pl.semaphore_signal(go_up.at[0], inc=1, device_id={"sub": me_z - 1}, device_id_type=MESH)
            pl.semaphore_signal(go_down.at[0], inc=1, device_id={"sub": me_z + 1}, device_id_type=MESH)
    for copy in small[:3]:
        copy.wait()
    load_scale.wait()

    owner = owner_ref[...]
    lanes = lax.broadcasted_iota(jnp.int32, (faces, faces), 1)
    rows = lax.broadcasted_iota(jnp.int32, (faces, faces), 0)
    earlier = jnp.where(rows < lanes, 1.0, 0.0).astype(BF16)
    padded = -(-subs // 16) * 16
    named = lax.broadcasted_iota(jnp.int32, (padded, faces), 0) == jnp.broadcast_to(
        owner, (padded, faces)
    )
    named = jnp.where(named, 1.0, 0.0)
    ranks = jnp.dot(named.astype(BF16), earlier, preferred_element_type=F32)
    rank = jnp.sum(named * ranks, axis=0, keepdims=True).astype(jnp.int32)
    sign = (1 - 2 * section_ref[0]).astype(F32)
    place = lax.broadcasted_iota(jnp.int32, (subs * room, faces), 0) == jnp.broadcast_to(
        owner * room + rank, (subs * room, faces)
    )
    packed[...] = jnp.dot(
        jnp.where(place, sign, 0.0).astype(BF16), scale_in[...], preferred_element_type=F32
    ).astype(BF16)
    spot = lax.broadcasted_iota(jnp.int32, (subs * 2 * room, faces), 0) == jnp.broadcast_to(
        (owner * 2 + me_f) * room + rank, (subs * 2 * room, faces)
    )
    slots = jnp.broadcast_to((slot_ref[...] + 1).astype(F32), (16, faces)).astype(BF16)
    coded = lax.dot_general(
        slots, jnp.where(spot, 1.0, 0.0).astype(BF16), (((1,), (1,)), ((), ())),
        preferred_element_type=F32,
    )
    for d in range(subs):
        codes_out[d] = coded[:1, d * 2 * room:(d + 1) * 2 * room]
    load_basis.wait()

    def start(copy):
        copy.start()

    def tell(semaphores, j, z):
        pl.semaphore_signal(
            semaphores.at[j - 2], inc=1, device_id={"sub": z}, device_id_type=MESH
        )

    def send(d):
        came = turn(me_z, d)
        start(remote(
            part(me_z, me_x, me_f, BASIS), part(me_z, me_x, me_f, BASIS),
            sent.at[BASIS], z_recv.at[came, BASIS], {"sub": d},
        ))
        share = shares[SCALE]
        mine = packed.at[pl.ds(pl.multiple_of(d * room + me_x * share, share), share), :]
        start(remote(
            mine, part(me_z, me_x, me_f, SCALE), sent.at[SCALE], z_recv.at[came, SCALE],
            {"sub": d},
        ))
        start(remote(
            codes_out.at[d], codes.at[me_z, me_f], sent.at[CODE], z_recv.at[came, CODE],
            {"sub": d},
        ))

    for j in range(2, subs):
        @pl.when(me_z - j >= 0)
        def _():
            pl.semaphore_wait(go_down.at[j - 2], 1)
            if j < subs - 1:
                @pl.when(me_z + 1 < subs)
                def _():
                    tell(go_down, j + 1, me_z + 1)
    for j in reversed(range(1, subs)):
        @pl.when(me_z - j >= 0)
        def _():
            send(me_z - j)
    for j in range(1, subs):
        @pl.when(me_z + j < subs)
        def _():
            if j > 1:
                pl.semaphore_wait(go_up.at[j - 2], 1)
                if j < subs - 1:
                    @pl.when(me_z >= 1)
                    def _():
                        tell(go_up, j + 1, me_z - 1)
            send(me_z + j)
    own_rows = pl.ds(pl.multiple_of(me_z * room, room), room)

    def own_part(f):
        return scales.at[me_z, pl.ds(pl.multiple_of(f * room, room), room), :]

    swaps = [
        remote(
            packed.at[own_rows, :], own_part(me_f), swap_sent.at[0], swap_recv.at[0],
            {"face": other_f},
        ),
        remote(
            codes_out.at[me_z], codes.at[me_z, me_f], swap_sent.at[1], swap_recv.at[1],
            {"face": other_f},
        ),
    ]
    for copy in swaps:
        copy.start()
    scales[me_z, pl.ds(pl.multiple_of(me_f * room, room), room), :] = packed[own_rows, :]
    codes[me_z, me_f] = codes_out[me_z]

    first = me_z * blocks + me_f * half
    for copy in small[3:]:
        copy.wait()
    load_mortar.wait()
    cell = row_to_column(cell_ref[...].astype(F32), cols).astype(jnp.int32)
    rate = row_to_column(rate_ref[...], cols)
    offset = (
        jnp.broadcast_to(cell, (cols, dofs))
        - lax.broadcasted_iota(jnp.int32, (cols, dofs), 1)
        - first * dofs
    )
    rates = jnp.broadcast_to(rate, (cols, dofs))

    @pl.loop(0, half)
    def _(b):
        term = jnp.where(offset == b * dofs, rates, 0.0)
        pumped[b] = (pumped[b].astype(F32) + term).astype(BF16)

    step = min(8, half)

    def weigh(z):
        code = jnp.broadcast_to(codes[z, 0] + codes[z, 1], (half, 2 * room)).astype(jnp.int32)
        targets = me_f * half + 1 + lax.broadcasted_iota(jnp.int32, (half, 2 * room), 0)
        picks = jnp.where(code == targets, 1.0, 0.0).astype(BF16)
        weights[...] = jnp.dot(picks, scales[z], preferred_element_type=F32)

    def compute(z, opening):
        weigh(z)

        def piece(i):
            rows = []
            for j in range(step):
                b = i * step + j
                rows.append((pumped[b].astype(F32) * weights[pl.ds(b, 1), :]).astype(BF16))
            flux = jnp.dot(
                jnp.concatenate(rows, axis=0), bases[z], preferred_element_type=F32
            )
            at = pl.ds(i * (step * cols), step * cols)
            if not opening:
                flux = flux + total[at, :]
            total[at, :] = flux

        for i in range(half // step):
            piece(i)

    remote(
        own_part(other_f), own_part(other_f), swap_sent.at[0], swap_recv.at[0], {"face": other_f}
    ).wait_recv()
    theirs = codes.at[me_z, other_f]
    remote(theirs, theirs, swap_sent.at[1], swap_recv.at[1], {"face": other_f}).wait_recv()
    compute(me_z, True)

    kinds = (BASIS, SCALE, CODE)

    def pass_on_z(k):
        z = in_turn(k)
        for kind in kinds:
            mine = part(z, me_x, me_f, kind)
            remote(
                mine, mine, sent.at[kind], z_recv.at[k - 1, kind], {"face": other_f}
            ).wait_recv()
            if kind != CODE:
                for dx in range(1, width):
                    x = lax.rem(me_x + dx, width)
                    start(remote(
                        mine, mine, sent.at[kind], x_recv.at[k - 1, dx - 1, kind], {"rhs": x}
                    ))
            start(remote(
                mine, mine, sent.at[kind], core_recv.at[k - 1, kind], {"face": other_f}
            ))

    def pass_on_x(k):
        z = in_turn(k)
        for kind in kinds[:2]:
            for dx in range(1, width):
                x = lax.rem(me_x + width - dx, width)
                came = part(z, x, me_f, kind)
                remote(
                    came, came, sent.at[kind], x_recv.at[k - 1, dx - 1, kind], {"face": other_f}
                ).wait_recv()
                start(remote(
                    came, came, sent.at[kind], core_recv.at[k - 1, kind], {"face": other_f}
                ))

    def arrive(k):
        z = in_turn(k)
        for kind in kinds:
            if kind == CODE:
                came = codes.at[z, other_f]
            else:
                rows = shares[kind] * width
                at = pl.ds(pl.multiple_of(other_f * rows, rows), rows)
                came = (bases if kind == BASIS else scales).at[z, at, :]
            remote(
                came, came, sent.at[kind], core_recv.at[k - 1, kind], {"face": other_f}
            ).wait_recv()
        return z

    for k in range(1, subs):
        pass_on_z(k)
    for k in range(1, subs):
        pass_on_x(k)
        if k > 1:
            z = arrive(k - 1)
            compute(z, False)
    last = arrive(subs - 1)
    weigh(last)
    basis_last[...] = bases[last]
    load_projection.wait()
    for copy in swaps:
        copy.wait_send()
    for kind, whole in ((BASIS, bases), (SCALE, scales), (CODE, codes)):
        whole = whole.at[pl.ds(0, subs - 1)]
        remote(
            whole, whole, sent.at[kind], core_recv.at[0, kind], {"face": other_f}
        ).wait_send()


def project(total, weights, pumped, basis_ref, projection_ref, out_ref, staged, sems):
    parts, tile, _ = staged.shape
    cols = pumped.shape[1]
    step = tile // cols
    copies = []
    for i in range(parts):
        at = pl.ds(i * tile, tile)
        rows = []
        for j in range(step):
            b = i * step + j
            rows.append((pumped[b].astype(F32) * weights[pl.ds(b, 1), :]).astype(BF16))
        summed = total[at, :] + jnp.dot(
            jnp.concatenate(rows, axis=0), basis_ref[...], preferred_element_type=F32
        )
        staged[i] = jnp.dot(
            summed.astype(BF16), projection_ref[...], preferred_element_type=F32
        )
        copies.append(pltpu.make_async_copy(staged.at[i], out_ref.at[at], sems.at[i]))
        copies[-1].start()
    for copy in copies:
        copy.wait()


def on_device(
    mortar_in, pump_rate, well_cell, face_owner, face_slot, face_scale, section, basis, projection
):
    blocks, cols, dofs = mortar_in.shape
    faces = face_slot.shape[0]
    subs, width = lax.axis_size("sub"), lax.axis_size("rhs")
    half = blocks // 2
    cap = min(faces, -(-2 * faces // subs))
    share = -(-cap // (16 * width)) * 16
    room = share * width
    assert subs > 1 and blocks < 256
    sizes = (subs, width, faces, blocks, cols, dofs, room)
    vmem = pl.BlockSpec(memory_space=pltpu.VMEM)
    hbm = pl.BlockSpec(memory_space=pl.ANY)
    dma = pltpu.SemaphoreType.DMA
    kept = pl.pallas_call(
        functools.partial(kernel, sizes),
        out_shape=(
            pltpu.VMEM((half * cols, dofs), F32),
            pltpu.VMEM((half, dofs), F32),
            pltpu.VMEM((half, cols, dofs), BF16),
            pltpu.VMEM((dofs, dofs), BF16),
            pltpu.VMEM((dofs, dofs), BF16),
        ),
        in_specs=[hbm] * 9,
        out_specs=(vmem,) * 5,
        scratch_shapes=[
            pltpu.VMEM((1, faces), jnp.int32),
            pltpu.VMEM((1, faces), jnp.int32),
            pltpu.SMEM((1,), jnp.int32),
            pltpu.VMEM((1, cols), jnp.int32),
            pltpu.VMEM((1, cols), F32),
            pltpu.VMEM((faces, dofs), BF16),
            pltpu.VMEM((subs * room, dofs), BF16),
            pltpu.VMEM((subs, 1, 2 * room), F32),
            pltpu.VMEM((subs, dofs, dofs), BF16),
            pltpu.VMEM((subs, 2 * room, dofs), BF16),
            pltpu.VMEM((subs, 2, 1, 2 * room), F32),
            dma((9,)), dma((3,)), dma((2,)), dma((2,)),
            dma((subs - 1, 3)), dma((subs - 1, max(width - 1, 1), 2)), dma((subs - 1, 3)),
            pltpu.SemaphoreType.REGULAR((max(subs - 2, 1),)),
            pltpu.SemaphoreType.REGULAR((max(subs - 2, 1),)),
        ],
        compiler_params=pltpu.CompilerParams(collective_id=0, has_side_effects=True),
    )(
        face_owner.reshape(1, faces), face_slot.reshape(1, faces), section,
        well_cell.reshape(1, cols), pump_rate.reshape(1, cols), mortar_in, face_scale, basis,
        projection,
    )
    rows = half * cols
    parts = 8
    result = pl.pallas_call(
        project,
        out_shape=jax.ShapeDtypeStruct((rows, dofs), F32),
        in_specs=[vmem] * 5,
        out_specs=hbm,
        scratch_shapes=[pltpu.VMEM((parts, rows // parts, dofs), F32), dma((parts,))],
    )(*(pltpu.with_memory_space_constraint(a, pltpu.VMEM) for a in kept))
    return result.reshape(half, cols, dofs)


def solution(mesh):
    in_specs = (
        P(("groups", "sub"), "rhs", None),
        P(("groups", "rhs")),
        P(("groups", "rhs")),
        P(("groups", "sub", "face"), None),
        P(("groups", "sub", "face")),
        P(("groups", "sub", "face"), None),
        P(("groups", "sub")),
        P(("groups", "sub"), None, None),
        P(),
    )
    out_specs = P(("groups", "sub", "face"), "rhs", None)
    return jax.shard_map(
        on_device, mesh=mesh, in_specs=in_specs, out_specs=out_specs, check_vma=False
    )
```
